1024 devices in a mesh: section: 64 (over y, x, core), tp: 16 (over z).
Axes of the slice: x: 4, y: 8, z: 16, core: 2. Of those that a mesh axis runs over, the one named last changes fastest.
Arguments:
- inputs: bfloat16 [64, 256, 8192], P('section', None, 'tp'), may hold values from -41 to 41, as said below
- norm_gain: bfloat16 [64, 8192], P('section', 'tp'), may hold values from 0.5 to 2
- w_value: bfloat16 [64, 8192, 512], P('section', 'tp'), may hold values from -0.0625 to 0.0625
- w_output: bfloat16 [64, 512, 8192], P('section', None, 'tp'), may hold values from -0.25 to 0.25
- moments: bfloat16 [64, 2, 8192], P('section', None, 'tp'), may hold values from 0.099609375 to 10
- capped: int32 [64], P('section'), may hold values from 0 to 1, as said below
Outputs:
- next_input: bfloat16 [64, 256, 8192], P('section', None, 'tp')
- guest_moments: bfloat16 [64, 2, 8192], P('section', None, 'tp')
The draws below stay inside these ranges and needn't reach their ends.
Inputs may be any that keep to these rules, and one draw needn't show every extreme that they name: `capped`: each entry is 0 or 1; the last section is never capped, no two neighbouring sections are both capped, and sections 0 and 62 are always capped. `inputs`: activations of mixed row and feature scales.
All inputs are finite; a program needn't handle non-finite values.
Results may differ from the reference program's by a relative error of at most 0.0042.
Values may be sent and summed in bfloat16 or wider, within the bound.
A program may use at most 32 MiB of HBM per device.

```python
import math
import jax
import jax.numpy as jnp
from jax import lax

D = 8192
KV = 512
TOK = 256
SECTIONS = 64
N_SECTION = 64


def draw_inputs(key, part):
    key_noise, key_rows, key_cols = jax.random.split(key, 3)
    full_shape = (SECTIONS, TOK, D)
    raw_noise = jnp.clip(jax.random.normal(key_noise, full_shape, jnp.float32), -4.0, 4.0)
    row_scale = jnp.exp(jax.random.uniform(key_rows, (SECTIONS, TOK, 1), jnp.float32, math.log(0.3), math.log(3.0)))
    col_scale = jnp.exp(jax.random.uniform(key_cols, (1, 1, D), jnp.float32, math.log(0.3), math.log(3.0)))
    return (raw_noise * row_scale * col_scale).astype(jnp.bfloat16)


def draw_capped(key, part):
    picks = jax.random.randint(key, (SECTIONS,), 0, 3)
    earlier = jnp.concatenate([jnp.ones((1,), jnp.int32), picks[:-1].astype(jnp.int32)])
    positions = jnp.arange(SECTIONS)
    forced = (positions == 0) | (positions == SECTIONS - 2)
    banned = (positions == 1) | (positions == SECTIONS - 3) | (positions == SECTIONS - 1)
    randomly = (picks == 0) & (earlier != 0) & jnp.logical_not(banned)
    return (forced | randomly).astype(jnp.int32)


def shard_levels(own_key, dims, pieces, smallest, top_value):
    def one(position, blocks):
        steps = jax.random.uniform(jax.random.fold_in(jax.random.fold_in(own_key, 6), position), (blocks,), jnp.float32, smallest / len(pieces), top_value / len(pieces))
        return jnp.repeat(jnp.exp(steps), dims[position] // blocks).reshape((-1,) + (1,) * (len(dims) - position - 1))

    loudness = one(*pieces[0])
    for cut in pieces[1:]:
        loudness = loudness * one(*cut)
    return loudness


def gaussian(own_key, extent, width, bound, cuts=(), held_as=jnp.bfloat16):
    result = jax.random.normal(own_key, extent, jnp.float32) * width
    if len(cuts) > 0:
        result = shard_levels(own_key, extent, cuts, -0.22, 0.18) * result
    return jnp.clip(result, min=-bound, max=bound).astype(held_as)


def setup_inputs(seed: int = 0) -> dict:
    keys = jax.random.split(jax.random.key(seed), 7)
    return {
        "inputs": draw_inputs(jax.random.fold_in(keys[6], 71), 0),
        "norm_gain": jnp.clip(jnp.exp(math.log(2.0) - 1.3862944 * jax.random.uniform(keys[1], (SECTIONS, D), jnp.float32) ** shard_levels(keys[1], (SECTIONS, D), ((0, 64), (1, 16)), -0.2, 0.2)), 0.5, 2.0).astype(jnp.bfloat16),
        "w_value": gaussian(keys[2], (SECTIONS, D, KV), D ** -0.5, 0.0625, ((0, 64), (1, 16))),
        "w_output": gaussian(keys[3], (SECTIONS, KV, D), KV ** -0.5, 0.25, ((0, 64), (2, 16))),
        "moments": jnp.clip(jnp.exp(math.log(10.0) - 4.609084 * jax.random.uniform(keys[4], (SECTIONS, 2, D), jnp.float32) ** shard_levels(keys[4], (SECTIONS, 2, D), ((0, 64), (2, 16)), -0.2, 0.2)), 0.099609375, 10.0).astype(jnp.bfloat16),
        "capped": draw_capped(jax.random.fold_in(keys[6], 71), 0),
    }


eps = 1e-05

def apply_layer(stream, gain_row, w_value, w_output, active):
    widened = stream.astype(jnp.float32)
    squares = lax.optimization_barrier(jnp.sum(widened * widened, axis=-1, keepdims=True))
    scaled = (widened * gain_row.astype(jnp.float32)).astype(jnp.bfloat16)
    projected = jnp.dot(scaled, w_value, preferred_element_type=jnp.float32)
    values = (projected * lax.rsqrt(squares / D + eps)).astype(jnp.bfloat16)
    update = jnp.dot(values, w_output, preferred_element_type=jnp.float32)
    return (widened + active * update).astype(jnp.bfloat16)

def reference(inputs, norm_gain, w_value, w_output, moments, capped):
    cap_flags = capped.astype(jnp.float32)

    def one_section(section_index):
        before = jnp.maximum(section_index - 1, 0).astype(jnp.int32)
        guest_flag = jnp.where(section_index > 0, cap_flags[before], jnp.zeros((), jnp.float32))
        middle = apply_layer(inputs[section_index], norm_gain[before], w_value[before], w_output[before], guest_flag)
        return apply_layer(middle, norm_gain[section_index], w_value[section_index], w_output[section_index], 1.0 - cap_flags[section_index])
    results = lax.map(one_section, jnp.arange(N_SECTION, dtype=jnp.int32))
    next_input = jnp.concatenate([jnp.zeros_like(results[:1]), results[:-1]], axis=0)
    guest_flags = jnp.concatenate([jnp.zeros((1,), jnp.float32), cap_flags[:-1]])
    shifted = jnp.concatenate([jnp.zeros_like(moments[:1]), moments[:-1]], axis=0)
    guest_moments = (shifted.astype(jnp.float32) * guest_flags[:, None, None]).astype(jnp.bfloat16)
    return (next_input, guest_moments)
```

```python
import functools

import jax
import jax.numpy as jnp
from jax import lax
from jax.experimental import pallas as pl
from jax.experimental.pallas import tpu as pltpu
from jax.sharding import PartitionSpec as P

MESH = pl.DeviceIdType.MESH
D = 8192
EPS = 1e-05
F32 = jnp.float32
BF16 = jnp.bfloat16

TREE = (
    (0, 6), (0, -6), (0, 3), (0, -3), (0, 1), (0, -1),
    (3, 4), (-3, -4), (3, 2), (-3, -2),
    (6, 8), (6, 7), (-6, -7), (6, 5), (-6, -5),
)
PARENT = {child: parent for parent, child in TREE}
CHILDREN = {node: [c for p, c in TREE if p == node] for node in range(-7, 9)}
RELAYS = (6, -6, 3, -3)
LEAVES = (8, 7, -7, 5, -5, 4, -4, 2, -2, 1, -1)
OFFSETS = sorted({c - p for p, c in TREE} | {p - c for p, c in TREE})


def kernel(
    tp, sections, tok, cuts,
    x_hbm, gain_ref, wv_hbm, wo_hbm, mom_ref, cap_ref,
    out_ref, gmom_ref,
    x, mid, wv, wo, wv_in, wo_in, small, small_in, scaled, values, res, *rest,
):
    chunks = len(cuts)
    channels = chunks + 1
    parts, got, relay = rest[:channels], rest[channels : 2 * channels], rest[2 * channels : 3 * channels]
    local_sem, sec_send, sec_recv, tree_send, tree_recv = rest[3 * channels :]
    me, sec = lax.axis_index("tp"), lax.axis_index("section")
    own = tok // tp
    following = lax.rem(sec + 1, sections)
    previous = lax.rem(sec + sections - 1, sections)

    def at(offset):
        return lax.rem(me + (offset + tp), tp)

    def block(offset):
        return pl.ds(pl.multiple_of(at(offset) * own, own), own)

    loads = [
        pltpu.make_async_copy(x_hbm.at[0], x, local_sem.at[0]),
        pltpu.make_async_copy(wv_hbm.at[0], wv, local_sem.at[1]),
        pltpu.make_async_copy(wo_hbm.at[0], wo, local_sem.at[2]),
    ]
    barrier = pltpu.get_barrier_semaphore()
    for offset in OFFSETS:
        pl.semaphore_signal(barrier, inc=1, device_id={"tp": at(offset)}, device_id_type=MESH)
    pl.semaphore_signal(barrier, inc=1, device_id={"section": following}, device_id_type=MESH)
    pl.semaphore_signal(barrier, inc=1, device_id={"section": previous}, device_id_type=MESH)
    for load in loads:
        load.start()
    cap = jnp.full((1, small.shape[1]), cap_ref[0].astype(F32), F32)
    small[0:1, :] = gain_ref[...].astype(F32)
    small[1:3, :] = mom_ref[0].astype(F32)
    small[3:4, :] = cap
    small[4:8, :] = jnp.zeros((4, small.shape[1]), F32)
    pl.semaphore_wait(barrier, len(OFFSETS) + 2)

    def onward(n, src, dst):
        return pltpu.make_async_remote_copy(
            src_ref=src, dst_ref=dst, send_sem=sec_send.at[n], recv_sem=sec_recv.at[n],
            device_id={"section": following}, device_id_type=MESH,
        )

    small_copy = onward(0, small, small_in)
    small_copy.start()
    wv_copies = []
    for n, (start, width) in enumerate(cuts):
        copy = onward(1 + n, wv_hbm.at[0, :, pl.ds(start, width)], wv_in.at[:, pl.ds(start, width)])
        copy.start()
        wv_copies.append(copy)
    wo_copy = onward(1 + chunks, wo_hbm.at[0], wo_in)
    wo_copy.start()

    def up(k, q, src):
        return pltpu.make_async_remote_copy(
            src_ref=src, dst_ref=got[k].at[q % tp], send_sem=tree_send.at[k, q % tp], recv_sem=tree_recv.at[k, q % tp],
            device_id={"tp": at(PARENT[q] - q)}, device_id_type=MESH,
        )

    def leaf_copy(k, q):
        return up(k, q, parts[k].at[block(-q), :])

    def leaves(k):
        for q in LEAVES:
            leaf_copy(k, q).start()

    def summed(k, p):
        total = parts[k][block(-p), :].astype(F32)
        for q in CHILDREN[p]:
            (leaf_copy(k, q) if q in LEAVES else up(k, q, relay[k].at[RELAYS.index(q)])).wait_recv()
            total = total + got[k][q % tp].astype(F32)
        return total

    def relays(k):
        for n, p in enumerate(RELAYS):
            relay[k][n] = summed(k, p).astype(BF16)
            up(k, p, relay[k].at[n]).start()

    def down(k, edge):
        p, q = edge
        rows = values.at[k - channels, block(-p), :]
        return pltpu.make_async_remote_copy(
            src_ref=rows, dst_ref=rows, send_sem=tree_send.at[k, q % tp], recv_sem=tree_recv.at[k, q % tp],
            device_id={"tp": at(q - p)}, device_id_type=MESH,
        )

    def spread(k):
        seen = {0}
        for edge in TREE:
            p = edge[0]
            if p not in seen:
                down(k, (PARENT[p], p)).wait_recv()
                seen.add(p)
            down(k, edge).start()
        for edge in TREE:
            if edge[1] not in seen:
                down(k, edge).wait_recv()

    def normalized(total, squares):
        return (total * lax.rsqrt(squares[:, 0:1] * (1.0 / D) + EPS)).astype(BF16)

    def squares_of(stream):
        return jnp.broadcast_to(jnp.sum(stream * stream, axis=-1, keepdims=True), (tok, 128))

    loads[0].wait()
    wide = x[...].astype(F32)
    first = cuts[0][1]
    parts[0][:, first:] = squares_of(wide).astype(BF16)
    small_copy.wait_recv()
    scaled[...] = (wide * small_in[0:1, :]).astype(BF16)
    guest = small_in[3:4, :] * jnp.where(sec > 0, 1.0, 0.0).astype(F32)
    gmom_ref[0] = (small_in[1:3, :] * guest).astype(BF16)
    for n, (start, width) in enumerate(cuts):
        wv_copies[n].wait_recv()
        parts[n][:, 0:width] = jnp.dot(
            scaled[...], wv_in[:, start : start + width], preferred_element_type=F32
        ).astype(BF16)
        leaves(n)
    totals = []
    for n in range(chunks):
        relays(n)
    for n in range(chunks):
        totals.append(summed(n, 0))
    squares = totals[0][:, first:]
    for n, (start, width) in enumerate(cuts):
        values[0, block(0), start : start + width] = normalized(totals[n][:, 0:width], squares)
    spread(channels)
    wo_copy.wait_recv()
    update = jnp.dot(values[0], wo_in[...], preferred_element_type=F32)
    mid[...] = (x[...].astype(F32) + guest * update).astype(BF16)

    k = chunks
    wide = mid[...].astype(F32)
    kv = wv.shape[1]
    parts[k][:, kv:] = squares_of(wide).astype(BF16)
    scaled[...] = (wide * small[0:1, :]).astype(BF16)
    loads[1].wait()
    parts[k][:, 0:kv] = jnp.dot(scaled[...], wv[...], preferred_element_type=F32).astype(BF16)
    leaves(k)
    relays(k)
    total = summed(k, 0)
    values[1, block(0), :] = normalized(total[:, 0:kv], total[:, kv:])
    spread(channels + 1)
    loads[2].wait()
    keep = sec < sections - 1
    out_copies = []
    pieces = 4
    rows = tok // pieces
    for n in range(pieces):
        span = pl.ds(n * rows, rows)
        update = jnp.dot(values[1, span, :], wo[...], preferred_element_type=F32)
        new = mid[span, :].astype(F32) + (1.0 - cap) * update
        res[span, :] = jnp.where(keep, new, 0.0).astype(BF16)
        copy = onward(2 + chunks + n, res.at[span, :], out_ref.at[0, span, :])
        copy.start()
        out_copies.append(copy)

    small_copy.wait_send()
    wo_copy.wait_send()
    for copy in wv_copies:
        copy.wait_send()
    for n in range(channels):
        for q in LEAVES:
            leaf_copy(n, q).wait_send()
        for r, p in enumerate(RELAYS):
            up(n, p, relay[n].at[r]).wait_send()
    for n in (channels, channels + 1):
        for edge in TREE:
            down(n, edge).wait_send()
    for copy in out_copies:
        copy.wait()


def on_device(tp, sections, inputs, norm_gain, w_value, w_output, moments, capped):
    tok, width = inputs.shape[1:]
    kv = w_value.shape[2]
    cuts = ((0, kv // 2), (kv // 2, kv // 2))
    widths = [w + (128 if n == 0 else 0) for n, (_, w) in enumerate(cuts)] + [kv + 128]
    channels = len(widths)
    own = tok // tp
    vmem, anywhere = pl.BlockSpec(memory_space=pltpu.VMEM), pl.BlockSpec(memory_space=pl.ANY)
    return pl.pallas_call(
        functools.partial(kernel, tp, sections, tok, cuts),
        out_shape=(
            jax.ShapeDtypeStruct(inputs.shape, BF16),
            jax.ShapeDtypeStruct(moments.shape, BF16),
        ),
        in_specs=[anywhere, vmem, anywhere, anywhere, vmem, pl.BlockSpec(memory_space=pltpu.SMEM)],
        out_specs=(anywhere, vmem),
        scratch_shapes=[
            pltpu.VMEM((tok, width), BF16),
            pltpu.VMEM((tok, width), BF16),
            pltpu.VMEM((width, kv), BF16),
            pltpu.VMEM((kv, width), BF16),
            pltpu.VMEM((width, kv), BF16),
            pltpu.VMEM((kv, width), BF16),
            pltpu.VMEM((8, width), F32),
            pltpu.VMEM((8, width), F32),
            pltpu.VMEM((tok, width), BF16),
            pltpu.VMEM((2, tok, kv), BF16),
            pltpu.VMEM((tok, width), BF16),
            *[pltpu.VMEM((tok, w), BF16) for w in widths],
            *[pltpu.VMEM((tp, own, w), BF16) for w in widths],
            *[pltpu.VMEM((len(RELAYS), own, w), BF16) for w in widths],
            pltpu.SemaphoreType.DMA((3,)),
            pltpu.SemaphoreType.DMA((channels + 5,)),
            pltpu.SemaphoreType.DMA((channels + 5,)),
            pltpu.SemaphoreType.DMA((channels + 2, tp)),
            pltpu.SemaphoreType.DMA((channels + 2, tp)),
        ],
        compiler_params=pltpu.CompilerParams(collective_id=0, has_side_effects=True),
    )(inputs, norm_gain, w_value, w_output, moments, capped)


def solution(mesh):
    return jax.shard_map(
        functools.partial(on_device, mesh.shape["tp"], mesh.shape["section"]),
        mesh=mesh,
        in_specs=(
            P("section", None, "tp"),
            P("section", "tp"),
            P("section", "tp", None),
            P("section", None, "tp"),
            P("section", None, "tp"),
            P("section"),
        ),
        out_specs=(P("section", None, "tp"), P("section", None, "tp")),
        check_vma=False,
    )
```

```python
import functools

import jax
import jax.numpy as jnp
from jax import lax
from jax.experimental import pallas as pl
from jax.experimental.pallas import tpu as pltpu
from jax.sharding import PartitionSpec as P

MESH = pl.DeviceIdType.MESH
D = 8192
EPS = 1e-05
F32 = jnp.float32
BF16 = jnp.bfloat16

TREE = (
    (0, 6), (0, -6), (0, 3), (0, -3), (0, 1), (0, -1),
    (3, 4), (-3, -4), (3, 2), (-3, -2),
    (6, 8), (6, 7), (-6, -7), (6, 5), (-6, -5),
)
PARENT = {child: parent for parent, child in TREE}
CHILDREN = {node: [c for p, c in TREE if p == node] for node in range(-7, 9)}
RELAYS = (6, -6, 3, -3)
LEAVES = (8, 7, -7, 5, -5, 4, -4, 2, -2, 1, -1)
NEAR, FAR = (-3, -2, -1, 0, 1, 2, 3, 4), (5, 6, 7, 8, -7, -6, -5, -4)
ORDER = NEAR + FAR
OFFSETS = sorted({c - p for p, c in TREE} | {p - c for p, c in TREE})


def kernel(
    tp, sections, tok,
    x_hbm, gain_hbm, wv_hbm, wo_hbm, mom_hbm, cap_hbm,
    out_ref, gmom_ref,
    x, guest, mid, wv, wo, values, res, gain_ref, mom_ref, cap_ref, gmom, *rest,
):
    parts, got, relay = rest[0:2], rest[2:4], rest[4:6]
    local_sem, send_sem, recv_sem, mid_send, mid_recv, out_send, out_recv, tree_send, tree_recv = rest[6:]
    me, sec = lax.axis_index("tp"), lax.axis_index("section")
    own = tok // tp
    kv = wv.shape[1]
    following = lax.rem(sec + 1, sections)
    previous = lax.rem(sec + sections - 1, sections)

    def at(offset):
        return lax.rem(me + (offset + tp), tp)

    def block(q):
        return pl.ds(pl.multiple_of(at(-q) * own, own), own)

    def slot(q):
        return pl.ds(ORDER.index(q) * own, own)

    def span(group):
        return pl.ds(ORDER.index(group[0]) * own, len(group) * own)

    def onward(src, dst, send, recv):
        return pltpu.make_async_remote_copy(
            src_ref=src, dst_ref=dst, send_sem=send, recv_sem=recv,
            device_id={"section": following}, device_id_type=MESH,
        )

    x_loads = [pltpu.make_async_copy(x_hbm.at[0, block(q), :], x.at[slot(q), :], local_sem.at[n]) for n, q in enumerate(ORDER)]
    loads = [
        pltpu.make_async_copy(wv_hbm.at[0], wv, local_sem.at[tp]),
        pltpu.make_async_copy(wo_hbm.at[0], wo, local_sem.at[tp + 1]),
    ]
    smalls = [
        pltpu.make_async_copy(gain_hbm, gain_ref, local_sem.at[tp + 2]),
        pltpu.make_async_copy(mom_hbm, mom_ref, local_sem.at[tp + 3]),
        pltpu.make_async_copy(cap_hbm, cap_ref, local_sem.at[tp + 4]),
    ]
    first, last = sec == 0, sec == sections - 1
    inner, outer = jnp.logical_not(first), jnp.logical_not(last)
    barrier = pltpu.get_barrier_semaphore()

    @pl.when(outer)
    def _():
        pl.semaphore_signal(barrier, inc=1, device_id={"section": following}, device_id_type=MESH)

    @pl.when(inner)
    def _():
        pl.semaphore_signal(barrier, inc=1, device_id={"section": previous}, device_id_type=MESH)

    for offset in OFFSETS:
        pl.semaphore_signal(barrier, inc=1, device_id={"tp": at(offset)}, device_id_type=MESH)
    for load in x_loads + smalls + loads:
        load.start()
    for load in x_loads:
        load.wait()

    @pl.when(jnp.logical_or(first, last))
    def _():
        pl.semaphore_wait(barrier, len(OFFSETS) + 1)

    @pl.when(jnp.logical_and(inner, outer))
    def _():
        pl.semaphore_wait(barrier, len(OFFSETS) + 2)

    def guest_copy(n, group):
        return pltpu.make_async_remote_copy(
            src_ref=x.at[span(group), :], dst_ref=guest.at[span(group), :], send_sem=send_sem.at[n], recv_sem=recv_sem.at[n],
            device_id={"section": previous}, device_id_type=MESH,
        )

    guest_copies = [guest_copy(n, group) for n, group in enumerate((FAR, NEAR))]

    @pl.when(inner)
    def _():
        for copy in guest_copies:
            copy.start()

    for load in smalls:
        load.wait()
    cap = jnp.full((1, x.shape[1]), cap_ref[0].astype(F32), F32)
    gain = gain_ref[...].astype(F32)
    gmom[...] = (mom_ref[0].astype(F32) * cap).astype(BF16)
    gmom_copy = onward(gmom, gmom_ref.at[0], send_sem.at[2], recv_sem.at[2])

    @pl.when(outer)
    def _():
        gmom_copy.start()

    @pl.when(first)
    def _():
        mid[...] = x[...]
        out_ref[...] = jnp.zeros_like(out_ref)
        gmom_ref[...] = jnp.zeros_like(gmom_ref)

    @pl.when(last)
    def _():
        guest[...] = x[...]

    def up(k, q, src):
        return pltpu.make_async_remote_copy(
            src_ref=src, dst_ref=got[k].at[q % tp], send_sem=tree_send.at[k, q % tp], recv_sem=tree_recv.at[k, q % tp],
            device_id={"tp": at(PARENT[q] - q)}, device_id_type=MESH,
        )

    def leaf_copy(k, q):
        return up(k, q, parts[k].at[slot(q), :])

    def down(k, edge):
        p, q = edge
        return pltpu.make_async_remote_copy(
            src_ref=values.at[k, slot(p), :], dst_ref=values.at[k, slot(q), :],
            send_sem=tree_send.at[2 + k, q % tp], recv_sem=tree_recv.at[2 + k, q % tp],
            device_id={"tp": at(q - p)}, device_id_type=MESH,
        )

    def project(k, group, stream):
        rows = span(group)
        total = jnp.sum(stream * stream, axis=-1, keepdims=True)
        parts[k][rows, kv:] = jnp.broadcast_to(total, (stream.shape[0], 128)).astype(BF16)
        parts[k][rows, 0:kv] = jnp.dot(
            (stream * gain).astype(BF16), wv[...], preferred_element_type=F32
        ).astype(BF16)
        for q in group:
            if q in LEAVES:
                leaf_copy(k, q).start()

    def summed(k, p):
        total = parts[k][slot(p), :].astype(F32)
        for q in CHILDREN[p]:
            (leaf_copy(k, q) if q in LEAVES else up(k, q, relay[k].at[RELAYS.index(q)])).wait_recv()
            total = total + got[k][q % tp].astype(F32)
        return total

    def gather(k, order):
        for p in order:
            n = RELAYS.index(p)
            relay[k][n] = summed(k, p).astype(BF16)
            up(k, p, relay[k].at[n]).start()
        total = summed(k, 0)
        squares = total[:, kv : kv + 1]
        values[k, slot(0), :] = (total[:, 0:kv] * lax.rsqrt(squares * (1.0 / D) + EPS)).astype(BF16)

    def spread(k):
        seen = {0}
        for edge in TREE:
            p = edge[0]
            if p not in seen:
                down(k, (PARENT[p], p)).wait_recv()
                seen.add(p)
            down(k, edge).start()
        return seen

    def updated(k, group, seen):
        for q in group:
            if q not in seen:
                down(k, (PARENT[q], q)).wait_recv()
        return jnp.dot(values[k, span(group), :], wo[...], preferred_element_type=F32)

    loads[0].wait()
    for copy, group in zip(guest_copies, (FAR, NEAR)):

        @pl.when(outer)
        def _():
            copy.wait_recv()

        project(0, group, guest[span(group), :].astype(F32))
    gather(0, RELAYS)
    seen = spread(0)
    loads[1].wait()
    mid_copies = []
    for n, group in enumerate((NEAR, FAR)):
        rows = span(group)
        update = updated(0, group, seen)
        res[0, rows, :] = (guest[rows, :].astype(F32) + cap * update).astype(BF16)
        copy = onward(res.at[0, rows, :], mid.at[rows, :], mid_send.at[n], mid_recv.at[n])
        mid_copies.append(copy)

        @pl.when(outer)
        def _():
            copy.start()

    for copy, group in zip(mid_copies, (NEAR, FAR)):

        @pl.when(inner)
        def _():
            copy.wait_recv()

        project(1, group, mid[span(group), :].astype(F32))
    gather(1, RELAYS[2:] + RELAYS[:2])
    seen = spread(1)
    out_copies = []
    for group in (NEAR, FAR):
        rows = span(group)
        update = updated(1, group, seen)
        res[1, rows, :] = (mid[rows, :].astype(F32) + (1.0 - cap) * update).astype(BF16)
        copies = [
            onward(res.at[1, slot(q), :], out_ref.at[0, block(q), :], out_send.at[ORDER.index(q)], out_recv.at[ORDER.index(q)])
            for q in group
        ]
        out_copies += copies

        @pl.when(outer)
        def _():
            for copy in copies:
                copy.start()

    @pl.when(outer)
    def _():
        for copy in [gmom_copy, *mid_copies, *out_copies]:
            copy.wait_send()

    @pl.when(inner)
    def _():
        for copy in guest_copies:
            copy.wait_send()

    for k in (0, 1):
        for q in LEAVES:
            leaf_copy(k, q).wait_send()
        for n, p in enumerate(RELAYS):
            up(k, p, relay[k].at[n]).wait_send()
        for edge in TREE:
            down(k, edge).wait_send()

    @pl.when(inner)
    def _():
        for copy in [gmom_copy, *out_copies]:
            copy.wait_recv()


def on_device(tp, sections, inputs, norm_gain, w_value, w_output, moments, capped):
    tok, width = inputs.shape[1:]
    kv = w_value.shape[2]
    own = tok // tp
    vmem, anywhere = pl.BlockSpec(memory_space=pltpu.VMEM), pl.BlockSpec(memory_space=pl.ANY)
    stream = pltpu.VMEM((tok, width), BF16)
    copies = pltpu.SemaphoreType.DMA
    return pl.pallas_call(
        functools.partial(kernel, tp, sections, tok),
        out_shape=(pltpu.VMEM(inputs.shape, BF16), pltpu.VMEM(moments.shape, BF16)),
        in_specs=[anywhere] * 6,
        out_specs=(vmem, vmem),
        scratch_shapes=[
            stream,
            stream,
            stream,
            pltpu.VMEM((width, kv), BF16),
            pltpu.VMEM((kv, width), BF16),
            pltpu.VMEM((2, tok, kv), BF16),
            pltpu.VMEM((2, tok, width), BF16),
            pltpu.VMEM(norm_gain.shape, BF16),
            pltpu.VMEM(moments.shape, BF16),
            pltpu.SMEM(capped.shape, jnp.int32),
            pltpu.VMEM(moments.shape[1:], BF16),
            *[pltpu.VMEM((tok, kv + 128), BF16)] * 2,
            *[pltpu.VMEM((tp, own, kv + 128), BF16)] * 2,
            *[pltpu.VMEM((len(RELAYS), own, kv + 128), BF16)] * 2,
            copies((tp + 5,)),
            copies((3,)),
            copies((3,)),
            copies((2,)),
            copies((2,)),
            copies((tp,)),
            copies((tp,)),
            copies((4, tp)),
            copies((4, tp)),
        ],
        compiler_params=pltpu.CompilerParams(collective_id=0, has_side_effects=True),
    )(inputs, norm_gain, w_value, w_output, moments, capped)


def solution(mesh):
    return jax.shard_map(
        functools.partial(on_device, mesh.shape["tp"], mesh.shape["section"]),
        mesh=mesh,
        in_specs=(
            P("section", None, "tp"),
            P("section", "tp"),
            P("section", "tp", None),
            P("section", None, "tp"),
            P("section", None, "tp"),
            P("section"),
        ),
        out_specs=(P("section", None, "tp"), P("section", None, "tp")),
        check_vma=False,
    )
```

```python
import functools

import jax
import jax.numpy as jnp
from jax import lax
from jax.experimental import pallas as pl
from jax.experimental.pallas import tpu as pltpu
from jax.sharding import PartitionSpec as P

MESH = pl.DeviceIdType.MESH
D = 8192
EPS = 1e-05
F32 = jnp.float32
BF16 = jnp.bfloat16

TREE = (
    (0, 6), (0, -6), (0, 3), (0, -3), (0, 1), (0, -1),
    (3, 4), (-3, -4), (3, 2), (-3, -2),
    (6, 8), (6, 7), (-6, -7), (6, 5), (-6, -5),
)
PARENT = {child: parent for parent, child in TREE}
CHILDREN = {node: [c for p, c in TREE if p == node] for node in range(-7, 9)}
RELAYS = (6, -6, 3, -3)
LEAVES = (8, 7, -7, 5, -5, 4, -4, 2, -2, 1, -1)
NEAR, FAR = (-3, -2, -1, 0, 1, 2, 3, 4), (5, 6, 7, 8, -7, -6, -5, -4)
ORDER = NEAR + FAR
HEADS = (6, -6, 3, -3, 1, -1, 0)
OFFSETS = sorted({c - p for p, c in TREE} | {p - c for p, c in TREE})


def kernel(
    tp, sections, tok,
    x_hbm, gain_hbm, wv_hbm, wo_hbm, mom_hbm, cap_hbm,
    out_ref, gmom_ref,
    x, guest, mid, mid_in, wv, wo_in, owned, values, gain_ref, mom_ref, cap_ref, gmom, flag, flag_in, *rest,
):
    parts, got, relay = rest[0:2], rest[2:4], rest[4:6]
    local_sem, send_sem, recv_sem, tree_send, tree_recv = rest[6:]
    me, sec = lax.axis_index("tp"), lax.axis_index("section")
    own = tok // tp
    kv = wv.shape[1]
    following = lax.rem(sec + 1, sections)
    previous = lax.rem(sec + sections - 1, sections)
    first, last = sec == 0, sec == sections - 1
    inner, outer = jnp.logical_not(first), jnp.logical_not(last)

    def at(offset):
        return lax.rem(me + (offset + tp), tp)

    def block(q):
        return pl.ds(pl.multiple_of(at(-q) * own, own), own)

    def slot(q):
        return pl.ds(ORDER.index(q) * own, own)

    def span(group):
        return pl.ds(ORDER.index(group[0]) * own, len(group) * own)

    def beside(n, src, dst, section):
        return pltpu.make_async_remote_copy(
            src_ref=src, dst_ref=dst, send_sem=send_sem.at[n], recv_sem=recv_sem.at[n],
            device_id={"section": section}, device_id_type=MESH,
        )

    x_loads = [pltpu.make_async_copy(x_hbm.at[0, block(q), :], x.at[slot(q), :], local_sem.at[n]) for n, q in enumerate(ORDER)]
    wv_load = pltpu.make_async_copy(wv_hbm.at[0], wv, local_sem.at[tp])
    smalls = [
        pltpu.make_async_copy(gain_hbm, gain_ref, local_sem.at[tp + 1]),
        pltpu.make_async_copy(mom_hbm, mom_ref, local_sem.at[tp + 2]),
        pltpu.make_async_copy(cap_hbm, cap_ref, local_sem.at[tp + 3]),
    ]
    barrier = pltpu.get_barrier_semaphore()

    @pl.when(inner)
    def _():
        for p in HEADS[::-1]:
            pl.semaphore_signal(barrier, inc=1, device_id={"section": previous, "tp": at(-p)}, device_id_type=MESH)

    @pl.when(outer)
    def _():
        for p in HEADS[::-1]:
            pl.semaphore_signal(barrier, inc=1, device_id={"section": following, "tp": at(p)}, device_id_type=MESH)

    for offset in OFFSETS:
        pl.semaphore_signal(barrier, inc=1, device_id={"tp": at(offset)}, device_id_type=MESH)
    for load in [*x_loads, wv_load, *smalls]:
        load.start()
    for load in x_loads:
        load.wait()

    @pl.when(jnp.logical_or(first, last))
    def _():
        pl.semaphore_wait(barrier, len(OFFSETS) + len(HEADS))

    @pl.when(jnp.logical_and(inner, outer))
    def _():
        pl.semaphore_wait(barrier, len(OFFSETS) + 2 * len(HEADS))

    guest_copies = [beside(n, x.at[span(g), :], guest.at[span(g), :], previous) for n, g in enumerate((FAR, NEAR))]

    @pl.when(inner)
    def _():
        for copy in guest_copies:
            copy.start()

    wo_copy = beside(2, wo_hbm.at[0], wo_in, following)

    @pl.when(outer)
    def _():
        wo_copy.start()

    for load in smalls:
        load.wait()
    cap = jnp.full(flag.shape, cap_ref[0].astype(F32), F32)
    flag[...] = cap
    gain = gain_ref[...].astype(F32)
    gmom[...] = (mom_ref[0].astype(F32) * cap[0:1, :]).astype(BF16)
    small_copies = [beside(3, flag, flag_in, following), beside(4, gmom, gmom_ref.at[0], following)]

    @pl.when(outer)
    def _():
        for copy in small_copies:
            copy.start()

    @pl.when(first)
    def _():
        mid[...] = x[...]
        out_ref[...] = jnp.zeros_like(out_ref)
        gmom_ref[...] = jnp.zeros_like(gmom_ref)

    @pl.when(last)
    def _():
        guest[...] = x[...]

    def up(k, q, src):
        return pltpu.make_async_remote_copy(
            src_ref=src, dst_ref=got[k].at[q % tp], send_sem=tree_send.at[k, q % tp], recv_sem=tree_recv.at[k, q % tp],
            device_id={"tp": at(PARENT[q] - q)}, device_id_type=MESH,
        )

    def leaf_copy(k, q):
        return up(k, q, parts[k].at[slot(q), :])

    def lead(k, q):
        return pltpu.make_async_remote_copy(
            src_ref=owned.at[k], dst_ref=values.at[k, slot(q), :],
            send_sem=tree_send.at[2 + k, q % tp], recv_sem=tree_recv.at[2 + k, q % tp],
            device_id={"section": following, "tp": at(q)}, device_id_type=MESH,
        )

    def down(k, edge):
        p, q = edge
        return pltpu.make_async_remote_copy(
            src_ref=values.at[k, slot(p), :], dst_ref=values.at[k, slot(q), :],
            send_sem=tree_send.at[2 + k, q % tp], recv_sem=tree_recv.at[2 + k, q % tp],
            device_id={"tp": at(q - p)}, device_id_type=MESH,
        )

    def project(k, group, stream):
        rows = span(group)
        total = jnp.sum(stream * stream, axis=-1, keepdims=True)
        parts[k][rows, kv:] = jnp.broadcast_to(total, (stream.shape[0], 128)).astype(BF16)
        parts[k][rows, 0:kv] = jnp.dot(
            (stream * gain).astype(BF16), wv[...], preferred_element_type=F32
        ).astype(BF16)
        for q in group:
            if q in LEAVES:
                leaf_copy(k, q).start()

    def summed(k, p):
        total = parts[k][slot(p), :].astype(F32)
        for q in CHILDREN[p]:
            (leaf_copy(k, q) if q in LEAVES else up(k, q, relay[k].at[RELAYS.index(q)])).wait_recv()
            total = total + got[k][q % tp].astype(F32)
        return total

    def pass_on(k, order):
        for p in order:
            n = RELAYS.index(p)
            relay[k][n] = summed(k, p).astype(BF16)
            up(k, p, relay[k].at[n]).start()

    def own_values(k):
        total = summed(k, 0)
        squares = total[:, kv : kv + 1]
        owned[k] = (total[:, 0:kv] * lax.rsqrt(squares * (1.0 / D) + EPS)).astype(BF16)

        @pl.when(outer)
        def _():
            for q in HEADS:
                lead(k, q).start()

    def forward(k):
        for p in RELAYS[2:] + RELAYS[:2]:
            lead(k, p).wait_recv()
            for q in CHILDREN[p]:
                down(k, (p, q)).start()

    def updated(k, group):
        for q in group:
            if q in HEADS:
                if q not in RELAYS:
                    lead(k, q).wait_recv()
            else:
                down(k, (PARENT[q], q)).wait_recv()
        return jnp.dot(values[k, span(group), :], wo_in[...], preferred_element_type=F32)

    wv_load.wait()
    for copy, group in zip(guest_copies, (FAR, NEAR)):

        @pl.when(outer)
        def _():
            copy.wait_recv()

        project(0, group, guest[span(group), :].astype(F32))
    pass_on(0, RELAYS)
    own_values(0)

    mid_copies = [beside(5 + n, mid.at[span(g), :], mid_in.at[span(g), :], following) for n, g in enumerate((NEAR, FAR))]

    @pl.when(inner)
    def _():
        forward(0)
        wo_copy.wait_recv()
        small_copies[0].wait_recv()

    for group in (NEAR, FAR):
        rows = span(group)

        @pl.when(inner)
        def _():
            mid[rows, :] = (x[rows, :].astype(F32) + flag_in[0:1, :] * updated(0, group)).astype(BF16)

        project(1, group, mid[rows, :].astype(F32))
        if group == NEAR:

            @pl.when(outer)
            def _():
                mid_copies[0].start()

    pass_on(1, RELAYS[2:] + RELAYS[:2])

    @pl.when(outer)
    def _():
        mid_copies[1].start()

    own_values(1)

    @pl.when(inner)
    def _():
        forward(1)
        for copy, group in zip(mid_copies, (NEAR, FAR)):
            copy.wait_recv()
            rows = span(group)
            new = mid_in[rows, :].astype(F32) + (1.0 - flag_in[0:1, :]) * updated(1, group)
            new = new.astype(BF16)
            for n, q in enumerate(group):
                out_ref[0, block(q), :] = new[n * own : (n + 1) * own, :]
        small_copies[1].wait_recv()
        for copy in guest_copies:
            copy.wait_send()
        for k in (0, 1):
            for p, q in TREE:
                if p != 0:
                    down(k, (p, q)).wait_send()

    @pl.when(outer)
    def _():
        for copy in [wo_copy, *small_copies, *mid_copies]:
            copy.wait_send()
        for k in (0, 1):
            for q in HEADS:
                lead(k, q).wait_send()

    for k in (0, 1):
        for q in LEAVES:
            leaf_copy(k, q).wait_send()
        for n, p in enumerate(RELAYS):
            up(k, p, relay[k].at[n]).wait_send()


def on_device(tp, sections, inputs, norm_gain, w_value, w_output, moments, capped):
    tok, width = inputs.shape[1:]
    kv = w_value.shape[2]
    own = tok // tp
    vmem, anywhere = pl.BlockSpec(memory_space=pltpu.VMEM), pl.BlockSpec(memory_space=pl.ANY)
    stream = pltpu.VMEM((tok, width), BF16)
    copies = pltpu.SemaphoreType.DMA
    return pl.pallas_call(
        functools.partial(kernel, tp, sections, tok),
        out_shape=(pltpu.VMEM(inputs.shape, BF16), pltpu.VMEM(moments.shape, BF16)),
        in_specs=[anywhere] * 6,
        out_specs=(vmem, vmem),
        scratch_shapes=[
            *[stream] * 4,
            pltpu.VMEM((width, kv), BF16),
            pltpu.VMEM((kv, width), BF16),
            pltpu.VMEM((2, own, kv), BF16),
            pltpu.VMEM((2, tok, kv), BF16),
            pltpu.VMEM(norm_gain.shape, BF16),
            pltpu.VMEM(moments.shape, BF16),
            pltpu.SMEM(capped.shape, jnp.int32),
            pltpu.VMEM(moments.shape[1:], BF16),
            *[pltpu.VMEM((8, width), F32)] * 2,
            *[pltpu.VMEM((tok, kv + 128), BF16)] * 2,
            *[pltpu.VMEM((tp, own, kv + 128), BF16)] * 2,
            *[pltpu.VMEM((len(RELAYS), own, kv + 128), BF16)] * 2,
            copies((tp + 4,)),
            copies((7,)),
            copies((7,)),
            copies((4, tp)),
            copies((4, tp)),
        ],
        compiler_params=pltpu.CompilerParams(collective_id=0, has_side_effects=True),
    )(inputs, norm_gain, w_value, w_output, moments, capped)


def solution(mesh):
    return jax.shard_map(
        functools.partial(on_device, mesh.shape["tp"], mesh.shape["section"]),
        mesh=mesh,
        in_specs=(
            P("section", None, "tp"),
            P("section", "tp"),
            P("section", "tp", None),
            P("section", None, "tp"),
            P("section", None, "tp"),
            P("section"),
        ),
        out_specs=(P("section", None, "tp"), P("section", None, "tp")),
        check_vma=False,
    )
```

```python
import functools

import jax
import jax.numpy as jnp
from jax import lax
from jax.experimental import pallas as pl
from jax.experimental.pallas import tpu as pltpu
from jax.sharding import PartitionSpec as P

MESH = pl.DeviceIdType.MESH
D = 8192
EPS = 1e-05
F32 = jnp.float32
BF16 = jnp.bfloat16

TREE = (
    (0, 5), (0, -5), (0, 2), (0, -2), (0, 1), (0, -1),
    (2, 3), (-2, -3),
    (5, 8), (5, 7), (-5, -7), (5, 6), (-5, -6), (5, 4), (-5, -4),
)
PARENT = {child: parent for parent, child in TREE}
CHILDREN = {node: [c for p, c in TREE if p == node] for node in range(-7, 9)}
RELAYS = (5, -5, 2, -2)
LEAVES = (8, 7, -7, 6, -6, 4, -4, 3, -3, 1, -1)
NEAR, FAR = (-3, -2, -1, 0, 1, 2, 3, 4), (5, 6, 7, 8, -7, -6, -5, -4)
ORDER = NEAR + FAR
HEADS = (5, -5, 2, -2, 1, -1, 0)
OFFSETS = sorted({c - p for p, c in TREE} | {p - c for p, c in TREE})


def kernel(
    tp, sections, tok,
    x_hbm, gain_hbm, wv_hbm, wo_hbm, mom_hbm, cap_hbm,
    out_ref, gmom_ref,
    x, guest, mid, mid_in, wv, wo_in, owned, values, gain_ref, mom_ref, cap_ref, gmom, flag, flag_in, *rest,
):
    parts, got, relay = rest[0:2], rest[2:4], rest[4:6]
    local_sem, send_sem, recv_sem, tree_send, tree_recv = rest[6:]
    me, sec = lax.axis_index("tp"), lax.axis_index("section")
    own = tok // tp
    kv = wv.shape[1]
    following = lax.rem(sec + 1, sections)
    previous = lax.rem(sec + sections - 1, sections)
    first, last = sec == 0, sec == sections - 1
    inner, outer = jnp.logical_not(first), jnp.logical_not(last)

    def at(offset):
        return lax.rem(me + (offset + tp), tp)

    def block(q):
        return pl.ds(pl.multiple_of(at(-q) * own, own), own)

    def slot(q):
        return pl.ds(ORDER.index(q) * own, own)

    def span(group):
        return pl.ds(ORDER.index(group[0]) * own, len(group) * own)

    def beside(n, src, dst, section):
        return pltpu.make_async_remote_copy(
            src_ref=src, dst_ref=dst, send_sem=send_sem.at[n], recv_sem=recv_sem.at[n],
            device_id={"section": section}, device_id_type=MESH,
        )

    x_loads = [pltpu.make_async_copy(x_hbm.at[0, block(q), :], x.at[slot(q), :], local_sem.at[n]) for n, q in enumerate(ORDER)]
    wv_load = pltpu.make_async_copy(wv_hbm.at[0], wv, local_sem.at[tp])
    smalls = [
        pltpu.make_async_copy(gain_hbm, gain_ref, local_sem.at[tp + 1]),
        pltpu.make_async_copy(mom_hbm, mom_ref, local_sem.at[tp + 2]),
        pltpu.make_async_copy(cap_hbm, cap_ref, local_sem.at[tp + 3]),
    ]
    barrier = pltpu.get_barrier_semaphore()

    @pl.when(inner)
    def _():
        for p in HEADS[::-1]:
            pl.semaphore_signal(barrier, inc=1, device_id={"section": previous, "tp": at(-p)}, device_id_type=MESH)

    @pl.when(outer)
    def _():
        for p in HEADS[::-1]:
            pl.semaphore_signal(barrier, inc=1, device_id={"section": following, "tp": at(p)}, device_id_type=MESH)

    for offset in OFFSETS:
        pl.semaphore_signal(barrier, inc=1, device_id={"tp": at(offset)}, device_id_type=MESH)
    for load in [*x_loads, wv_load, *smalls]:
        load.start()
    for load in x_loads:
        load.wait()

    @pl.when(jnp.logical_or(first, last))
    def _():
        pl.semaphore_wait(barrier, len(OFFSETS) + len(HEADS))

    @pl.when(jnp.logical_and(inner, outer))
    def _():
        pl.semaphore_wait(barrier, len(OFFSETS) + 2 * len(HEADS))

    guest_copies = [beside(n, x.at[span(g), :], guest.at[span(g), :], previous) for n, g in enumerate((FAR, NEAR))]

    @pl.when(inner)
    def _():
        for copy in guest_copies:
            copy.start()

    wo_copy = beside(2, wo_hbm.at[0], wo_in, following)

    @pl.when(outer)
    def _():
        wo_copy.start()

    for load in smalls:
        load.wait()
    cap = jnp.full(flag.shape, cap_ref[0].astype(F32), F32)
    flag[...] = cap
    gain = gain_ref[...].astype(F32)
    gmom[...] = (mom_ref[0].astype(F32) * cap[0:1, :]).astype(BF16)
    small_copies = [beside(3, flag, flag_in, following), beside(4, gmom, gmom_ref.at[0], following)]

    @pl.when(outer)
    def _():
        for copy in small_copies:
            copy.start()

    @pl.when(first)
    def _():
        mid[...] = x[...]
        out_ref[...] = jnp.zeros_like(out_ref)
        gmom_ref[...] = jnp.zeros_like(gmom_ref)

    @pl.when(last)
    def _():
        guest[...] = x[...]

    def up(k, q, src):
        return pltpu.make_async_remote_copy(
            src_ref=src, dst_ref=got[k].at[q % tp], send_sem=tree_send.at[k, q % tp], recv_sem=tree_recv.at[k, q % tp],
            device_id={"tp": at(PARENT[q] - q)}, device_id_type=MESH,
        )

    def leaf_copy(k, q):
        return up(k, q, parts[k].at[slot(q), :])

    def lead(k, q):
        return pltpu.make_async_remote_copy(
            src_ref=owned.at[k], dst_ref=values.at[k, slot(q), :],
            send_sem=tree_send.at[2 + k, q % tp], recv_sem=tree_recv.at[2 + k, q % tp],
            device_id={"section": following, "tp": at(q)}, device_id_type=MESH,
        )

    def down(k, edge):
        p, q = edge
        return pltpu.make_async_remote_copy(
            src_ref=values.at[k, slot(p), :], dst_ref=values.at[k, slot(q), :],
            send_sem=tree_send.at[2 + k, q % tp], recv_sem=tree_recv.at[2 + k, q % tp],
            device_id={"tp": at(q - p)}, device_id_type=MESH,
        )

    def project(k, group, stream):
        rows = span(group)
        total = jnp.sum(stream * stream, axis=-1, keepdims=True)
        parts[k][rows, kv:] = jnp.broadcast_to(total, (stream.shape[0], 128)).astype(BF16)
        parts[k][rows, 0:kv] = jnp.dot(
            (stream * gain).astype(BF16), wv[...], preferred_element_type=F32
        ).astype(BF16)
        for q in group:
            if q in LEAVES:
                leaf_copy(k, q).start()

    def summed(k, p):
        total = parts[k][slot(p), :].astype(F32)
        for q in CHILDREN[p]:
            (leaf_copy(k, q) if q in LEAVES else up(k, q, relay[k].at[RELAYS.index(q)])).wait_recv()
            total = total + got[k][q % tp].astype(F32)
        return total

    def pass_on(k, order):
        for p in order:
            n = RELAYS.index(p)
            relay[k][n] = summed(k, p).astype(BF16)
            up(k, p, relay[k].at[n]).start()

    def own_values(k):
        total = summed(k, 0)
        squares = total[:, kv : kv + 1]
        owned[k] = (total[:, 0:kv] * lax.rsqrt(squares * (1.0 / D) + EPS)).astype(BF16)

        @pl.when(outer)
        def _():
            for q in HEADS:
                lead(k, q).start()

    def forward(k):
        for p in RELAYS[2:] + RELAYS[:2]:
            lead(k, p).wait_recv()
            for q in CHILDREN[p]:
                down(k, (p, q)).start()

    def updated(k, group):
        for q in group:
            if q in HEADS:
                if q not in RELAYS:
                    lead(k, q).wait_recv()
            else:
                down(k, (PARENT[q], q)).wait_recv()
        return jnp.dot(values[k, span(group), :], wo_in[...], preferred_element_type=F32)

    wv_load.wait()
    for copy, group in zip(guest_copies, (FAR, NEAR)):

        @pl.when(outer)
        def _():
            copy.wait_recv()

        project(0, group, guest[span(group), :].astype(F32))
    pass_on(0, RELAYS)
    own_values(0)

    mid_copies = [beside(5 + n, mid.at[span(g), :], mid_in.at[span(g), :], following) for n, g in enumerate((NEAR, FAR))]

    @pl.when(inner)
    def _():
        forward(0)
        wo_copy.wait_recv()
        small_copies[0].wait_recv()

    for group in (NEAR, FAR[:4], FAR[4:]):
        rows = span(group)

        @pl.when(inner)
        def _():
            mid[rows, :] = (x[rows, :].astype(F32) + flag_in[0:1, :] * updated(0, group)).astype(BF16)

        project(1, group, mid[rows, :].astype(F32))
        if group == NEAR:

            @pl.when(outer)
            def _():
                mid_copies[0].start()

    pass_on(1, RELAYS[2:] + RELAYS[:2])

    @pl.when(outer)
    def _():
        mid_copies[1].start()

    own_values(1)

    @pl.when(inner)
    def _():
        forward(1)
        for copy, group in zip(mid_copies, (NEAR, FAR)):
            copy.wait_recv()
            rows = span(group)
            new = mid_in[rows, :].astype(F32) + (1.0 - flag_in[0:1, :]) * updated(1, group)
            new = new.astype(BF16)
            for n, q in enumerate(group):
                out_ref[0, block(q), :] = new[n * own : (n + 1) * own, :]
        small_copies[1].wait_recv()
        for copy in guest_copies:
            copy.wait_send()
        for k in (0, 1):
            for p, q in TREE:
                if p != 0:
                    down(k, (p, q)).wait_send()

    @pl.when(outer)
    def _():
        for copy in [wo_copy, *small_copies, *mid_copies]:
            copy.wait_send()
        for k in (0, 1):
            for q in HEADS:
                lead(k, q).wait_send()

    for k in (0, 1):
        for q in LEAVES:
            leaf_copy(k, q).wait_send()
        for n, p in enumerate(RELAYS):
            up(k, p, relay[k].at[n]).wait_send()


def on_device(tp, sections, inputs, norm_gain, w_value, w_output, moments, capped):
    tok, width = inputs.shape[1:]
    kv = w_value.shape[2]
    own = tok // tp
    vmem, anywhere = pl.BlockSpec(memory_space=pltpu.VMEM), pl.BlockSpec(memory_space=pl.ANY)
    stream = pltpu.VMEM((tok, width), BF16)
    copies = pltpu.SemaphoreType.DMA
    return pl.pallas_call(
        functools.partial(kernel, tp, sections, tok),
        out_shape=(pltpu.VMEM(inputs.shape, BF16), pltpu.VMEM(moments.shape, BF16)),
        in_specs=[anywhere] * 6,
        out_specs=(vmem, vmem),
        scratch_shapes=[
            *[stream] * 4,
            pltpu.VMEM((width, kv), BF16),
            pltpu.VMEM((kv, width), BF16),
            pltpu.VMEM((2, own, kv), BF16),
            pltpu.VMEM((2, tok, kv), BF16),
            pltpu.VMEM(norm_gain.shape, BF16),
            pltpu.VMEM(moments.shape, BF16),
            pltpu.SMEM(capped.shape, jnp.int32),
            pltpu.VMEM(moments.shape[1:], BF16),
            *[pltpu.VMEM((8, width), F32)] * 2,
            *[pltpu.VMEM((tok, kv + 128), BF16)] * 2,
            *[pltpu.VMEM((tp, own, kv + 128), BF16)] * 2,
            *[pltpu.VMEM((len(RELAYS), own, kv + 128), BF16)] * 2,
            copies((tp + 4,)),
            copies((7,)),
            copies((7,)),
            copies((4, tp)),
            copies((4, tp)),
        ],
        compiler_params=pltpu.CompilerParams(collective_id=0, has_side_effects=True),
    )(inputs, norm_gain, w_value, w_output, moments, capped)


def solution(mesh):
    return jax.shard_map(
        functools.partial(on_device, mesh.shape["tp"], mesh.shape["section"]),
        mesh=mesh,
        in_specs=(
            P("section", None, "tp"),
            P("section", "tp"),
            P("section", "tp", None),
            P("section", None, "tp"),
            P("section", None, "tp"),
            P("section"),
        ),
        out_specs=(P("section", None, "tp"), P("section", None, "tp")),
        check_vma=False,
    )
```

```python
import functools

import jax
import jax.numpy as jnp
from jax import lax
from jax.experimental import pallas as pl
from jax.experimental.pallas import tpu as pltpu
from jax.sharding import PartitionSpec as P

MESH = pl.DeviceIdType.MESH
D = 8192
EPS = 1e-05
F32 = jnp.float32
BF16 = jnp.bfloat16

TREE = (
    (0, 5), (0, -5), (0, 2), (0, -2), (0, 1), (0, -1),
    (2, 4), (-2, -4), (2, 3), (-2, -3),
    (5, 8), (5, 7), (-5, -7), (5, 6), (-5, -6),
)
PARENT = {child: parent for parent, child in TREE}
CHILDREN = {node: [c for p, c in TREE if p == node] for node in range(-7, 9)}
RELAYS = (5, -5, 2, -2)
LEAVES = (8, 7, -7, 6, -6, 4, -4, 3, -3, 1, -1)
NEAR, FAR = (-3, -2, -1, 0, 1, 2, 3, 4), (5, 6, 7, 8, -7, -6, -5, -4)
ORDER = NEAR + FAR
HEADS = (5, -5, 2, -2, 1, -1, 0)
OFFSETS = sorted({c - p for p, c in TREE} | {p - c for p, c in TREE})


def kernel(
    tp, sections, tok,
    x_hbm, gain_hbm, wv_hbm, wo_hbm, mom_hbm, cap_hbm,
    out_ref, gmom_ref,
    x, guest, mid, mid_in, wv, wo_in, owned, values, gain_ref, mom_ref, cap_ref, gmom, flag, flag_in, *rest,
):
    parts, got, relay = rest[0:2], rest[2:4], rest[4:6]
    local_sem, send_sem, recv_sem, tree_send, tree_recv = rest[6:]
    me, sec = lax.axis_index("tp"), lax.axis_index("section")
    own = tok // tp
    kv = wv.shape[1]
    following = lax.rem(sec + 1, sections)
    previous = lax.rem(sec + sections - 1, sections)
    first, last = sec == 0, sec == sections - 1
    inner, outer = jnp.logical_not(first), jnp.logical_not(last)

    def at(offset):
        return lax.rem(me + (offset + tp), tp)

    def block(q):
        return pl.ds(pl.multiple_of(at(-q) * own, own), own)

    def slot(q):
        return pl.ds(ORDER.index(q) * own, own)

    def span(group):
        return pl.ds(ORDER.index(group[0]) * own, len(group) * own)

    def beside(n, src, dst, section):
        return pltpu.make_async_remote_copy(
            src_ref=src, dst_ref=dst, send_sem=send_sem.at[n], recv_sem=recv_sem.at[n],
            device_id={"section": section}, device_id_type=MESH,
        )

    x_loads = [pltpu.make_async_copy(x_hbm.at[0, block(q), :], x.at[slot(q), :], local_sem.at[n]) for n, q in enumerate(ORDER)]
    wv_load = pltpu.make_async_copy(wv_hbm.at[0], wv, local_sem.at[tp])
    smalls = [
        pltpu.make_async_copy(gain_hbm, gain_ref, local_sem.at[tp + 1]),
        pltpu.make_async_copy(mom_hbm, mom_ref, local_sem.at[tp + 2]),
        pltpu.make_async_copy(cap_hbm, cap_ref, local_sem.at[tp + 3]),
    ]
    barrier = pltpu.get_barrier_semaphore()

    @pl.when(inner)
    def _():
        for p in HEADS[::-1]:
            pl.semaphore_signal(barrier, inc=1, device_id={"section": previous, "tp": at(-p)}, device_id_type=MESH)

    @pl.when(outer)
    def _():
        for p in HEADS[::-1]:
            pl.semaphore_signal(barrier, inc=1, device_id={"section": following, "tp": at(p)}, device_id_type=MESH)

    for offset in OFFSETS:
        pl.semaphore_signal(barrier, inc=1, device_id={"tp": at(offset)}, device_id_type=MESH)
    for load in [*x_loads, wv_load, *smalls]:
        load.start()
    for load in x_loads:
        load.wait()

    @pl.when(jnp.logical_or(first, last))
    def _():
        pl.semaphore_wait(barrier, len(OFFSETS) + len(HEADS))

    @pl.when(jnp.logical_and(inner, outer))
    def _():
        pl.semaphore_wait(barrier, len(OFFSETS) + 2 * len(HEADS))

    guest_copies = [beside(n, x.at[span(g), :], guest.at[span(g), :], previous) for n, g in ((0, FAR[:4]), (1, FAR[4:]), (7, NEAR))]

    @pl.when(inner)
    def _():
        for copy in guest_copies:
            copy.start()

    wo_copy = beside(2, wo_hbm.at[0], wo_in, following)

    @pl.when(outer)
    def _():
        wo_copy.start()

    for load in smalls:
        load.wait()
    cap = jnp.full(flag.shape, cap_ref[0].astype(F32), F32)
    flag[...] = cap
    gain = gain_ref[...].astype(F32)
    gmom[...] = (mom_ref[0].astype(F32) * cap[0:1, :]).astype(BF16)
    small_copies = [beside(3, flag, flag_in, following), beside(4, gmom, gmom_ref.at[0], following)]

    @pl.when(outer)
    def _():
        for copy in small_copies:
            copy.start()

    @pl.when(first)
    def _():
        mid[...] = x[...]
        out_ref[...] = jnp.zeros_like(out_ref)
        gmom_ref[...] = jnp.zeros_like(gmom_ref)

    @pl.when(last)
    def _():
        guest[...] = x[...]

    def up(k, q, src):
        return pltpu.make_async_remote_copy(
            src_ref=src, dst_ref=got[k].at[q % tp], send_sem=tree_send.at[k, q % tp], recv_sem=tree_recv.at[k, q % tp],
            device_id={"tp": at(PARENT[q] - q)}, device_id_type=MESH,
        )

    def leaf_copy(k, q):
        return up(k, q, parts[k].at[slot(q), :])

    def lead(k, q):
        return pltpu.make_async_remote_copy(
            src_ref=owned.at[k], dst_ref=values.at[k, slot(q), :],
            send_sem=tree_send.at[2 + k, q % tp], recv_sem=tree_recv.at[2 + k, q % tp],
            device_id={"section": following, "tp": at(q)}, device_id_type=MESH,
        )

    def down(k, edge):
        p, q = edge
        return pltpu.make_async_remote_copy(
            src_ref=values.at[k, slot(p), :], dst_ref=values.at[k, slot(q), :],
            send_sem=tree_send.at[2 + k, q % tp], recv_sem=tree_recv.at[2 + k, q % tp],
            device_id={"tp": at(q - p)}, device_id_type=MESH,
        )

    def project(k, group, stream):
        rows = span(group)
        total = jnp.sum(stream * stream, axis=-1, keepdims=True)
        parts[k][rows, kv:] = jnp.broadcast_to(total, (stream.shape[0], 128)).astype(BF16)
        parts[k][rows, 0:kv] = jnp.dot(
            (stream * gain).astype(BF16), wv[...], preferred_element_type=F32
        ).astype(BF16)
        for q in group:
            if q in LEAVES:
                leaf_copy(k, q).start()

    def summed(k, p):
        total = parts[k][slot(p), :].astype(F32)
        for q in CHILDREN[p]:
            (leaf_copy(k, q) if q in LEAVES else up(k, q, relay[k].at[RELAYS.index(q)])).wait_recv()
            total = total + got[k][q % tp].astype(F32)
        return total

    def pass_on(k, order):
        for p in order:
            n = RELAYS.index(p)
            relay[k][n] = summed(k, p).astype(BF16)
            up(k, p, relay[k].at[n]).start()

    def own_values(k):
        total = summed(k, 0)
        squares = total[:, kv : kv + 1]
        owned[k] = (total[:, 0:kv] * lax.rsqrt(squares * (1.0 / D) + EPS)).astype(BF16)

        @pl.when(outer)
        def _():
            for q in HEADS:
                lead(k, q).start()

    def forward(k):
        for p in RELAYS[2:] + RELAYS[:2]:
            lead(k, p).wait_recv()
            for q in CHILDREN[p]:
                down(k, (p, q)).start()

    def updated(k, group):
        for q in group:
            if q in HEADS:
                if q not in RELAYS:
                    lead(k, q).wait_recv()
            else:
                down(k, (PARENT[q], q)).wait_recv()
        return jnp.dot(values[k, span(group), :], wo_in[...], preferred_element_type=F32)

    wv_load.wait()
    for copy, group in zip(guest_copies, (FAR[:4], FAR[4:], NEAR)):

        @pl.when(outer)
        def _():
            copy.wait_recv()

        project(0, group, guest[span(group), :].astype(F32))
    pass_on(0, RELAYS)
    own_values(0)

    mid_copies = [beside(5 + n, mid.at[span(g), :], mid_in.at[span(g), :], following) for n, g in enumerate((NEAR, FAR))]

    @pl.when(inner)
    def _():
        forward(0)
        wo_copy.wait_recv()
        small_copies[0].wait_recv()

    for group in (NEAR, FAR[:4], FAR[4:]):
        rows = span(group)

        @pl.when(inner)
        def _():
            mid[rows, :] = (x[rows, :].astype(F32) + flag_in[0:1, :] * updated(0, group)).astype(BF16)

        project(1, group, mid[rows, :].astype(F32))
        if group == NEAR:

            @pl.when(outer)
            def _():
                mid_copies[0].start()

    pass_on(1, RELAYS[2:] + RELAYS[:2])

    @pl.when(outer)
    def _():
        mid_copies[1].start()

    own_values(1)

    @pl.when(inner)
    def _():
        forward(1)
        for copy, group in zip(mid_copies, (NEAR, FAR)):
            copy.wait_recv()
            rows = span(group)
            new = mid_in[rows, :].astype(F32) + (1.0 - flag_in[0:1, :]) * updated(1, group)
            new = new.astype(BF16)
            for n, q in enumerate(group):
                out_ref[0, block(q), :] = new[n * own : (n + 1) * own, :]
        small_copies[1].wait_recv()
        for copy in guest_copies:
            copy.wait_send()
        for k in (0, 1):
            for p, q in TREE:
                if p != 0:
                    down(k, (p, q)).wait_send()

    @pl.when(outer)
    def _():
        for copy in [wo_copy, *small_copies, *mid_copies]:
            copy.wait_send()
        for k in (0, 1):
            for q in HEADS:
                lead(k, q).wait_send()

    for k in (0, 1):
        for q in LEAVES:
            leaf_copy(k, q).wait_send()
        for n, p in enumerate(RELAYS):
            up(k, p, relay[k].at[n]).wait_send()


def on_device(tp, sections, inputs, norm_gain, w_value, w_output, moments, capped):
    tok, width = inputs.shape[1:]
    kv = w_value.shape[2]
    own = tok // tp
    vmem, anywhere = pl.BlockSpec(memory_space=pltpu.VMEM), pl.BlockSpec(memory_space=pl.ANY)
    stream = pltpu.VMEM((tok, width), BF16)
    copies = pltpu.SemaphoreType.DMA
    return pl.pallas_call(
        functools.partial(kernel, tp, sections, tok),
        out_shape=(pltpu.VMEM(inputs.shape, BF16), pltpu.VMEM(moments.shape, BF16)),
        in_specs=[anywhere] * 6,
        out_specs=(vmem, vmem),
        scratch_shapes=[
            *[stream] * 4,
            pltpu.VMEM((width, kv), BF16),
            pltpu.VMEM((kv, width), BF16),
            pltpu.VMEM((2, own, kv), BF16),
            pltpu.VMEM((2, tok, kv), BF16),
            pltpu.VMEM(norm_gain.shape, BF16),
            pltpu.VMEM(moments.shape, BF16),
            pltpu.SMEM(capped.shape, jnp.int32),
            pltpu.VMEM(moments.shape[1:], BF16),
            *[pltpu.VMEM((8, width), F32)] * 2,
            *[pltpu.VMEM((tok, kv + 128), BF16)] * 2,
            *[pltpu.VMEM((tp, own, kv + 128), BF16)] * 2,
            *[pltpu.VMEM((len(RELAYS), own, kv + 128), BF16)] * 2,
            copies((tp + 4,)),
            copies((8,)),
            copies((8,)),
            copies((4, tp)),
            copies((4, tp)),
        ],
        compiler_params=pltpu.CompilerParams(collective_id=0, has_side_effects=True),
    )(inputs, norm_gain, w_value, w_output, moments, capped)


def solution(mesh):
    return jax.shard_map(
        functools.partial(on_device, mesh.shape["tp"], mesh.shape["section"]),
        mesh=mesh,
        in_specs=(
            P("section", None, "tp"),
            P("section", "tp"),
            P("section", "tp", None),
            P("section", None, "tp"),
            P("section", None, "tp"),
            P("section"),
        ),
        out_specs=(P("section", None, "tp"), P("section", None, "tp")),
        check_vma=False,
    )
```
